512 devices in a mesh: box: 64 (over y, x, core), samp: 8 (over z).
Axes of the slice: x: 4, y: 8, z: 8, core: 2. Of those that a mesh axis runs over, the one named last changes fastest.
Arguments:
- currents: bfloat16 [2048, 8, 128], P(('box', 'samp')), may hold values from -6 to 6
- radiation: bfloat16 [2048, 2, 2, 512, 128], P(('box', 'samp')), may hold values from -0.1875 to 0.1875
- near_blocks: bfloat16 [2048, 8, 2, 128, 128], P(('box', 'samp')), may hold values from -0.125 to 0.125
- near_src: int32 [2048, 8], P(('box', 'samp')), may hold values from 0 to 2047, as said below
- leaf_parent: int32 [2048], P('box'), may hold values from 0 to 1023, as said below
- leaf_shift: int32 [2048], P('box'), may hold values from 0 to 7
- shift_table: bfloat16 [8, 2, 8192], P(None, None, 'samp'), may hold values from -4 to 4
- interp_idx: int32 [64, 2], P('samp'), may hold values from 0 to 3, as said below
- interp_val: bfloat16 [64, 2, 128, 128], P('samp'), may hold values from -0.375 to 0.375
- top_src: int32 [1024, 16], P('box'), may hold values from 0 to 1023, as said below
- top_disp: int32 [1024, 16], P('box'), may hold values from 0 to 31
- trans_table: bfloat16 [32, 2, 8192], P(None, None, 'samp'), may hold values from -1 to 1
Outputs:
- matvec: float32 [2048, 8, 128], P(('box', 'samp'))
The draws below stay inside these ranges and needn't reach their ends.
Inputs may be any that keep to these rules, and one draw needn't show every extreme that they name: `near_src`: entry 0 of a leaf's row is the leaf itself; every entry lies in the 4 leaves of the leaf's own device or of the devices just before and after it in box+samp order (leaves numbered box-major), and these ends are reached. `leaf_parent`: the parent of leaf l lies in its box group: its value divided by 16 equals l divided by 32. `interp_idx`: the 2 entries of a row differ. `top_src`: a source of top box t is another box of t's group (t // 16), or one of the last 8 boxes of the group before it, or one of the first 8 boxes of the group after it; both rims are reached.
All inputs are finite; a program needn't handle non-finite values.
Results may differ from the reference program's by a relative error of at most 0.013.
Values may be sent and summed in bfloat16 or wider, within the bound.
A program may use at most 64 MiB of HBM per device.

```python
import jax
import jax.numpy as jnp
from jax import lax

EXC = 4
UNK = 128
KL = 512
KT = 8192
BLK = 128
IBLK = 2
NEAR = 8
ILIST = 16
NSHIFT = 8
NDISP = 32
LEAF_DEV = 4
TOP_DEV = 16
RIM = 8
GROUP_LEAVES = 32
NL = 2048
NT = 1024
N_SAMP = 8


def draw_near_src(key, part):
    leaves = jnp.arange(NL)
    first = leaves // LEAF_DEV * LEAF_DEV
    offsets = jax.random.randint(jax.random.fold_in(key, 11), (NL, NEAR - 1), -LEAF_DEV, 2 * LEAF_DEV)
    lowest = leaves % LEAF_DEV == 0
    highest = leaves % LEAF_DEV == LEAF_DEV - 1
    column_low = jnp.where(lowest, -LEAF_DEV, offsets[:, 0])
    column_high = jnp.where(highest, 2 * LEAF_DEV - 1, offsets[:, 1])
    flipped = jax.random.randint(jax.random.fold_in(key, 13), (NL,), 0, 2) == 1
    column_one = jnp.where(flipped, column_high, column_low)
    column_two = jnp.where(flipped, column_low, column_high)
    offsets = jnp.concatenate([column_one[:, None], column_two[:, None], offsets[:, 2:]], axis=1)
    sources = jnp.clip(first[:, None] + offsets, 0, NL - 1)
    return jnp.concatenate([leaves[:, None], sources], axis=1).astype(jnp.int32)


def draw_leaf_parent(key, part):
    leaves = jnp.arange(NL)
    group_index = leaves // GROUP_LEAVES
    choice_top = jax.random.randint(jax.random.fold_in(key, 23), (NL,), 0, TOP_DEV)
    return (group_index * TOP_DEV + choice_top).astype(jnp.int32)


def draw_interp_idx(key, part):
    block_rows = KT // BLK
    in_blocks = KL // BLK
    scores = jax.random.randint(jax.random.fold_in(key, 37), (block_rows, in_blocks), 0, 4096) * 64 + jnp.arange(in_blocks)[None, :]
    order = jnp.argsort(scores, axis=1, stable=True)
    return order[:, :IBLK].astype(jnp.int32)


def draw_top_src(key, part):
    targets = jnp.arange(NT)
    group_index = targets // TOP_DEV
    local = targets % TOP_DEV
    group_total = NT // TOP_DEV
    side = jax.random.randint(jax.random.fold_in(key, 41), (NT, ILIST), 0, 3) - 1
    side = jnp.where((group_index[:, None] == 0) & (side == -1), 0, side)
    side = jnp.where((group_index[:, None] == group_total - 1) & (side == 1), 0, side)
    step_own = jax.random.randint(jax.random.fold_in(key, 43), (NT, ILIST), 0, TOP_DEV - 1)
    own = group_index[:, None] * TOP_DEV + (local[:, None] + 1 + step_own) % TOP_DEV
    picks = jax.random.randint(jax.random.fold_in(key, 47), (NT, ILIST), 0, RIM)
    lower = (group_index[:, None] - 1) * TOP_DEV + TOP_DEV - RIM + picks
    upper = (group_index[:, None] + 1) * TOP_DEV + picks
    sources = jnp.where(side == -1, lower, jnp.where(side == 1, upper, own))
    force_low = (local == 0) & (group_index > 0)
    force_high = (local == TOP_DEV - 1) & (group_index < group_total - 1)
    column_low = jnp.where(force_low, (group_index - 1) * TOP_DEV + TOP_DEV - RIM, sources[:, 0])
    column_high = jnp.where(force_high, (group_index + 1) * TOP_DEV + RIM - 1, sources[:, 1])
    sources = jnp.concatenate([column_low[:, None], column_high[:, None], sources[:, 2:]], axis=1)
    return sources.astype(jnp.int32)


def place_ends(entries, key, smallest, high):
    extent = entries.shape
    place = [jax.random.randint(jax.random.fold_in(key, axis), (), 0, extent[axis]) for axis in range(len(extent))]
    entries = entries.at[tuple(place)].set(smallest)
    longest = extent.index(max(extent))
    place[longest] = (place[longest] + 1) % extent[longest]
    return entries.at[tuple(place)].set(high)


def steps_of(rng, extent, split, low, high):
    factor_of, own = 1.0, jax.random.fold_in(rng, 6)
    for position, blocks in split:
        draws = jnp.exp(jax.random.uniform(jax.random.fold_in(own, position), (blocks,), jnp.float32, low / len(split), high / len(split)))
        factor_of = factor_of * jnp.repeat(draws, extent[position] // blocks).reshape([-1 if axis == position else 1 for axis in range(len(extent))])
    return factor_of


def centred(key, shape, scale, most, split=(), dtype=jnp.bfloat16):
    level = steps_of(key, shape, split, -0.22, 0.18) if split else 1.0
    drawn = jax.random.normal(key, shape, jnp.float32) * scale * level
    return jnp.minimum(jnp.maximum(drawn, -most), most).astype(dtype)


def setup_inputs(seed: int = 0) -> dict:
    key_list = jax.random.split(jax.random.key(seed), 13)
    currents = centred(key_list[0], (NL, 2 * EXC, UNK), 1.0, 6.0, ((0, 512),))
    radiation = centred(key_list[1], (NL, 2, 2, KL, UNK), (2 * KL) ** -0.5, 0.1875, ((0, 512),))
    near_blocks = centred(key_list[2], (NL, NEAR, 2, UNK, UNK), (2 * NEAR * UNK) ** -0.5, 0.125, ((0, 512),))
    near_src = draw_near_src(jax.random.fold_in(key_list[12], 71), 0)
    leaf_parent = draw_leaf_parent(jax.random.fold_in(key_list[12], 71), 0)
    leaf_shift = place_ends(jax.random.randint(key_list[5], (NL,), 0, NSHIFT), jax.random.fold_in(key_list[5], 1), 0, NSHIFT - 1).astype(jnp.int32)
    shift_table = centred(key_list[6], (NSHIFT, 2, KT), 0.5, 4.0, ((2, 8),))
    interp_idx = draw_interp_idx(jax.random.fold_in(key_list[12], 71), 0)
    interp_val = centred(key_list[8], (KT // BLK, IBLK, BLK, BLK), (IBLK * BLK) ** -0.5, 0.375, ((0, 8),))
    top_src = draw_top_src(jax.random.fold_in(key_list[12], 71), 0)
    top_disp = place_ends(jax.random.randint(key_list[10], (NT, ILIST), 0, NDISP), jax.random.fold_in(key_list[10], 1), 0, NDISP - 1).astype(jnp.int32)
    trans_table = centred(key_list[11], (NDISP, 2, KT), (2 * ILIST) ** -0.5, 1.0, ((2, 8),))
    return {"currents": currents, "radiation": radiation, "near_blocks": near_blocks, "near_src": near_src, "leaf_parent": leaf_parent, "leaf_shift": leaf_shift, "shift_table": shift_table, "interp_idx": interp_idx, "interp_val": interp_val, "top_src": top_src, "top_disp": top_disp, "trans_table": trans_table}


HIGHEST = lax.Precision.HIGHEST


def complex_mul(a_real, a_imag, b_real, b_imag):
    return a_real * b_real - a_imag * b_imag, a_real * b_imag + a_imag * b_real


def reference(currents, radiation, near_blocks, near_src, leaf_parent, leaf_shift, shift_table, interp_idx, interp_val, top_src, top_disp, trans_table):
    comps = 4 * EXC
    half_comp = 2 * EXC
    groups = NT // TOP_DEV
    in_blocks = KL // BLK
    range_blocks = KT // BLK // N_SAMP

    def radiate_one(packed):
        rad_leaf, cur_leaf = packed
        rad_leaf = rad_leaf.astype(jnp.float32)
        cur_leaf = cur_leaf.astype(jnp.float32)
        rad_real = rad_leaf[:, 0]
        rad_imag = rad_leaf[:, 1]
        cur_real = cur_leaf[:EXC]
        cur_imag = cur_leaf[EXC:]
        form = "pqu,eu->peq"
        out_real = jnp.einsum(form, rad_real, cur_real) - jnp.einsum(form, rad_imag, cur_imag)
        out_imag = jnp.einsum(form, rad_real, cur_imag) + jnp.einsum(form, rad_imag, cur_real)
        return jnp.concatenate([out_real.reshape(half_comp, KL), out_imag.reshape(half_comp, KL)], axis=0).astype(jnp.bfloat16)

    leaf_pat = lax.map(radiate_one, (radiation, currents))
    val_float = interp_val.astype(jnp.float32)

    def up_group(packed):
        patterns, parents, shifts, group_index = packed
        picked = patterns.reshape(GROUP_LEAVES, comps, in_blocks, BLK)[:, :, interp_idx, :].astype(jnp.float32)
        moved = jnp.einsum("lcbri,brki->lcbk", picked, val_float).reshape(GROUP_LEAVES, comps, KT)
        shift_rows = shift_table[shifts].astype(jnp.float32)
        up_real, up_imag = complex_mul(moved[:, :half_comp], moved[:, half_comp:], shift_rows[:, 0:1], shift_rows[:, 1:2])
        shifted = jnp.concatenate([up_real, up_imag], axis=1)
        member = (parents[None, :] - group_index * TOP_DEV == jnp.arange(TOP_DEV)[:, None]).astype(jnp.float32)
        return jnp.einsum("tl,lck->tck", member, shifted, precision=HIGHEST).astype(jnp.bfloat16)

    group_ids = jnp.arange(groups).astype(jnp.int32)
    top_pat = lax.map(up_group, (leaf_pat.reshape(groups, GROUP_LEAVES, comps, KL), leaf_parent.reshape(groups, GROUP_LEAVES), leaf_shift.reshape(groups, GROUP_LEAVES), group_ids))
    top_pat = top_pat.reshape(NT, comps, KT)
    block_onehot = (interp_idx[:, :, None] == jnp.arange(in_blocks)[None, None, :]).astype(jnp.float32).reshape(N_SAMP, range_blocks, IBLK, in_blocks)
    val_ranges = val_float.reshape(N_SAMP, range_blocks, IBLK, BLK, BLK)

    def down_group(packed):
        sources, displace, parents, shifts, group_index = packed

        def add_entry(entry, total):
            source_rows = top_pat[sources[:, entry]].astype(jnp.float32)
            coeff = trans_table[displace[:, entry]].astype(jnp.float32)
            part_real, part_imag = complex_mul(coeff[:, 0:1], coeff[:, 1:2], source_rows[:, :half_comp], source_rows[:, half_comp:])
            return total + jnp.concatenate([part_real, part_imag], axis=1)

        incoming = lax.fori_loop(0, ILIST, add_entry, jnp.zeros((TOP_DEV, comps, KT), jnp.float32)).astype(jnp.bfloat16)
        spread = incoming[parents - group_index * TOP_DEV].astype(jnp.float32)
        shift_rows = shift_table[shifts].astype(jnp.float32)
        down_real, down_imag = complex_mul(shift_rows[:, 0:1], -shift_rows[:, 1:2], spread[:, :half_comp], spread[:, half_comp:])
        down = jnp.concatenate([down_real, down_imag], axis=1).astype(jnp.bfloat16).astype(jnp.float32)
        parts = jnp.einsum("lcsbk,sbrki->lcsbri", down.reshape(GROUP_LEAVES, comps, N_SAMP, range_blocks, BLK), val_ranges)
        folded = jnp.einsum("lcsbri,sbrq->lcsqi", parts, block_onehot, precision=HIGHEST)
        rounded = lax.optimization_barrier(folded.astype(jnp.bfloat16)).astype(jnp.float32)
        return jnp.sum(rounded, axis=2).reshape(GROUP_LEAVES, comps, KL).astype(jnp.bfloat16)

    far = lax.map(down_group, (top_src.reshape(groups, TOP_DEV, ILIST), top_disp.reshape(groups, TOP_DEV, ILIST), leaf_parent.reshape(groups, GROUP_LEAVES), leaf_shift.reshape(groups, GROUP_LEAVES), group_ids))
    far = far.reshape(NL, comps, KL)

    def leaf_out(packed):
        rad_leaf, far_leaf, blocks, sources = packed
        rad_leaf = rad_leaf.astype(jnp.float32)
        far_leaf = far_leaf.astype(jnp.float32)
        rad_real = rad_leaf[:, 0]
        rad_imag = rad_leaf[:, 1]
        far_real = far_leaf[:half_comp].reshape(2, EXC, KL)
        far_imag = far_leaf[half_comp:].reshape(2, EXC, KL)
        form = "pqu,peq->eu"
        recv_real = jnp.einsum(form, rad_real, far_real) + jnp.einsum(form, rad_imag, far_imag)
        recv_imag = jnp.einsum(form, rad_real, far_imag) - jnp.einsum(form, rad_imag, far_real)
        near_rows = currents[sources].astype(jnp.float32)
        blocks = blocks.astype(jnp.float32)
        form_near = "nuv,nev->eu"
        near_real = jnp.einsum(form_near, blocks[:, 0], near_rows[:, :EXC]) - jnp.einsum(form_near, blocks[:, 1], near_rows[:, EXC:])
        near_imag = jnp.einsum(form_near, blocks[:, 0], near_rows[:, EXC:]) + jnp.einsum(form_near, blocks[:, 1], near_rows[:, :EXC])
        return jnp.concatenate([recv_real + near_real, recv_imag + near_imag], axis=0)

    return lax.map(leaf_out, (radiation, far, near_blocks, near_src))
```

```python
import functools

import jax
import jax.numpy as jnp
from jax import lax
from jax.experimental import pallas as pl
from jax.experimental.pallas import tpu as pltpu
from jax.sharding import PartitionSpec as P

MESH = pl.DeviceIdType.MESH
F32 = jnp.float32
BF16 = jnp.bfloat16
EXC = 4
COMPS = 16
HALF = 8
KL = 512
KD = 1024
BLK = 128
CH = 4
KC = KD // CH
LEAF = 4
SAMP = 8
GL = LEAF * SAMP
TOP = 16
RIM = 8
NEAR = 8
ILIST = 16
NDISP = 32
NSHIFT = 8

O_ORDER = 0
O_CONT = 32
O_LAST = 64
O_HAS = 80
O_SHIFT = 96
O_PARENT = 128
O_NEAR = 160
O_INTERP = 192
O_SRC = 208
O_DISP = 464
N_INTS = 720

NT_DIMS = (((1,), (1,)), ((), ()))
NN_DIMS = (((1,), (0,)), ((), ()))


def dot(a, b, dims):
    return lax.dot_general(a, b, dims, preferred_element_type=F32)


def kernel(
    boxes,
    ints,
    cur_hbm,
    rad_hbm,
    near_hbm,
    shift_hbm,
    val_hbm,
    trans_hbm,
    out_ref,
    nbr,
    xbuf,
    rad,
    near,
    shift_raw,
    val,
    trans_raw,
    w,
    sh,
    tr,
    own,
    ag_r,
    ag_l,
    ag_f,
    shifted,
    seg,
    topbf,
    halo_l,
    halo_r,
    srcf,
    inc,
    down,
    part,
    rs_r,
    rs_l,
    st_r,
    st_l,
    nearacc,
    local_sem,
    cur_sem,
    ag_send,
    ag_recv,
    halo_send,
    halo_recv,
    rs_send,
    rs_recv,
):
    box = lax.axis_index("box")
    samp = lax.axis_index("samp")
    total = boxes * SAMP
    right = (box, lax.rem(samp + 1, SAMP))
    left = (box, lax.rem(samp + SAMP - 1, SAMP))
    box_next = (lax.rem(box + 1, boxes), samp)
    box_prev = (lax.rem(box + boxes - 1, boxes), samp)
    flat = box * SAMP + samp
    flat_up = lax.rem(flat + 1, total)
    flat_dn = lax.rem(flat + total - 1, total)
    dev_up = (flat_up // SAMP, lax.rem(flat_up, SAMP))
    dev_dn = (flat_dn // SAMP, lax.rem(flat_dn, SAMP))

    barrier = pltpu.get_barrier_semaphore()
    for dev in (right, left, box_next, box_prev, dev_up, dev_dn):
        pl.semaphore_signal(barrier, inc=1, device_id=dev, device_id_type=MESH)

    def local(src, dst, index):
        return pltpu.make_async_copy(src, dst, local_sem.at[index])

    cur_copy = local(cur_hbm, nbr.at[pl.ds(LEAF, LEAF)], 0)
    rad_copies = [local(rad_hbm.at[i], rad.at[i], 1 + i) for i in range(LEAF)]
    val_copy = local(val_hbm, val, 5)
    shift_copy = local(shift_hbm, shift_raw, 6)
    trans_copy = local(trans_hbm, trans_raw, 7)
    near_copies = [local(near_hbm.at[i], near.at[i], 8 + i) for i in range(LEAF)]
    cur_copy.start()
    for copy in rad_copies:
        copy.start()
    val_copy.start()
    shift_copy.start()
    trans_copy.start()
    for copy in near_copies:
        copy.start()

    def remote(src, dst, send, recv, dev):
        return pltpu.make_async_remote_copy(
            src_ref=src,
            dst_ref=dst,
            send_sem=send,
            recv_sem=recv,
            device_id=dev,
            device_id_type=MESH,
        )

    def gather_copy(way, step, i):
        buf = ag_r if way == 0 else ag_l
        if step == 0:
            src = own.at[i]
        else:
            src = buf.at[step - 1, i]
        dst = ag_f.at[i] if step == 3 else buf.at[step, i]
        return remote(
            src, dst, ag_send.at[way, step, i], ag_recv.at[way, step, i], (right, left)[way]
        )

    def gather_has(way, step, i):
        return step < 3 or (i < 2) == (way == 0)

    gathers = {
        (way, step, i): gather_copy(way, step, i)
        for step in range(4)
        for i in range(LEAF)
        for way in range(2)
        if gather_has(way, step, i)
    }

    cur_copy.wait()
    for i in range(LEAF):
        x = nbr[LEAF + i].astype(F32)
        c_re, c_im = x[:EXC], x[EXC:]
        zero = jnp.zeros_like(c_re)
        lhs = jnp.concatenate(
            [
                jnp.concatenate([c_re, zero, c_im, zero], axis=0),
                jnp.concatenate([-c_im, zero, c_re, zero], axis=0),
                jnp.concatenate([zero, c_re, zero, c_im], axis=0),
                jnp.concatenate([zero, -c_im, zero, c_re], axis=0),
            ],
            axis=1,
        ).astype(BF16)
        rad_copies[i].wait()
        cat = jnp.concatenate([rad[i, p, r] for p in range(2) for r in range(2)], axis=1)
        own[i] = dot(lhs, cat, NT_DIMS).astype(BF16)
        if i == 0:
            pl.semaphore_wait(barrier, 6)
        gathers[0, 0, i].start()
        gathers[1, 0, i].start()

    cur_up = remote(cur_hbm, nbr.at[pl.ds(0, LEAF)], cur_sem.at[0], cur_sem.at[2], dev_up)
    cur_dn = remote(
        cur_hbm, nbr.at[pl.ds(2 * LEAF, LEAF)], cur_sem.at[1], cur_sem.at[3], dev_dn
    )
    cur_up.start()
    cur_dn.start()

    val_copy.wait()
    for b in range(KD // BLK):
        first = ints[O_INTERP + 2 * b]
        second = ints[O_INTERP + 2 * b + 1]
        for q in range(KL // BLK):
            tile = jnp.where(
                first == q,
                val[b, 0],
                jnp.where(second == q, val[b, 1], jnp.zeros((BLK, BLK), BF16)),
            )
            w[pl.ds(b * BLK, BLK), pl.ds(q * BLK, BLK)] = tile
    shift_copy.wait()
    for n in range(NSHIFT):
        row = shift_raw[n].astype(F32)
        for c in range(CH):
            for r in range(2):
                sh[c, n, r] = jnp.broadcast_to(
                    row[r : r + 1, c * KC : (c + 1) * KC], (HALF, KC)
                )

    def lift(rows, first_leaf):
        for c in range(CH):
            moved = dot(rows, w[pl.ds(c * KC, KC), :], NT_DIMS)
            for i in range(LEAF):
                leaf = first_leaf + i
                turn = ints[O_SHIFT + leaf]
                s_re = sh[c, turn, 0]
                s_im = sh[c, turn, 1]
                m_re = moved[i * COMPS : i * COMPS + HALF]
                m_im = moved[i * COMPS + HALF : (i + 1) * COMPS]
                shifted[c, leaf, 0:HALF] = m_re * s_re - m_im * s_im
                shifted[c, leaf, HALF:COMPS] = m_re * s_im + m_im * s_re

    def rows_of(block):
        return block.reshape(LEAF * COMPS, KL)

    def block_of(offset):
        return lax.rem(samp + offset + SAMP, SAMP)

    lift(rows_of(own[...]), block_of(0) * LEAF)

    def near_leaf(i):
        near_copies[i].wait()
        acc = jnp.zeros((HALF, BLK), F32)
        for n in range(NEAR):
            lhs = xbuf[ints[O_NEAR + i * NEAR + n]]
            acc += dot(lhs, jnp.concatenate([near[i, n, 0], near[i, n, 1]], axis=1), NT_DIMS)
        nearacc[i] = acc

    def expand_trans():
        trans_copy.wait()

        def body(n, carry):
            row = trans_raw[n].astype(F32)
            for c in range(CH):
                for r in range(2):
                    tr[c, n, r] = jnp.broadcast_to(
                        row[r : r + 1, c * KC : (c + 1) * KC], (HALF, KC)
                    )
            return carry

        lax.fori_loop(0, NDISP, body, 0)

    for step in range(3):
        for i in range(LEAF):
            for way in range(2):
                gathers[way, step, i].wait_recv()
                if gather_has(way, step + 1, i):
                    gathers[way, step + 1, i].start()
        lift(rows_of(ag_r[step]), block_of(-1 - step) * LEAF)
        lift(rows_of(ag_l[step]), block_of(1 + step) * LEAF)
        if step == 0:
            cur_up.wait_recv()
            cur_dn.wait_recv()
            for m in range(3 * LEAF):
                x = nbr[m].astype(F32)
                turned = jnp.concatenate([-x[EXC:], x[:EXC]], axis=0)
                xbuf[m] = jnp.concatenate([x, turned], axis=1).astype(BF16)
            expand_trans()
        elif step == 1:
            near_leaf(0)
            near_leaf(1)
        else:
            near_leaf(2)
            near_leaf(3)
    for i in range(LEAF):
        way = 0 if i < 2 else 1
        gathers[way, 3, i].wait_recv()
    lift(rows_of(ag_f[...]), block_of(4) * LEAF)

    halos = []
    for c in range(CH):

        def sum_step(j, acc):
            keep = ints[O_CONT + j]
            value = shifted[c, ints[O_ORDER + j]]
            acc = jnp.where(keep == 1, acc, jnp.zeros_like(acc)) + value
            seg[j] = acc
            return acc

        lax.fori_loop(0, GL, sum_step, jnp.zeros((COMPS, KC), F32), unroll=4)

        def top_step(t, carry):
            value = seg[ints[O_LAST + t]]
            value = jnp.where(ints[O_HAS + t] == 1, value, jnp.zeros_like(value)).astype(BF16)
            topbf[c, t] = value
            srcf[c, RIM + t] = value.astype(F32)
            return carry

        lax.fori_loop(0, TOP, top_step, 0, unroll=4)
        up = remote(
            topbf.at[c, pl.ds(TOP - RIM, RIM)],
            halo_l.at[c],
            halo_send.at[0, c],
            halo_recv.at[0, c],
            box_next,
        )
        dn = remote(
            topbf.at[c, pl.ds(0, RIM)],
            halo_r.at[c],
            halo_send.at[1, c],
            halo_recv.at[1, c],
            box_prev,
        )
        up.start()
        dn.start()
        halos.append((up, dn))

    for c in range(CH):
        halos[c][0].wait_recv()
        halos[c][1].wait_recv()

        def widen(t, carry):
            srcf[c, t] = halo_l[c, t].astype(F32)
            srcf[c, RIM + TOP + t] = halo_r[c, t].astype(F32)
            return carry

        lax.fori_loop(0, RIM, widen, 0, unroll=2)

        def move(t, carry):
            acc_re = jnp.zeros((HALF, KC), F32)
            acc_im = jnp.zeros((HALF, KC), F32)
            for j in range(ILIST):
                source = ints[O_SRC + t * ILIST + j]
                disp = ints[O_DISP + t * ILIST + j]
                s_re = srcf[c, source, 0:HALF]
                s_im = srcf[c, source, HALF:COMPS]
                t_re = tr[c, disp, 0]
                t_im = tr[c, disp, 1]
                acc_re += t_re * s_re - t_im * s_im
                acc_im += t_re * s_im + t_im * s_re
            value = jnp.concatenate([acc_re, acc_im], axis=0)
            inc[t] = value.astype(BF16).astype(F32)
            return carry

        lax.fori_loop(0, TOP, move, 0)

        def lower(leaf, carry):
            value = inc[ints[O_PARENT + leaf]]
            turn = ints[O_SHIFT + leaf]
            s_re = sh[c, turn, 0]
            s_im = sh[c, turn, 1]
            v_re, v_im = value[:HALF], value[HALF:]
            d_re = s_re * v_re + s_im * v_im
            d_im = s_re * v_im - s_im * v_re
            down[leaf, :, c * KC : (c + 1) * KC] = jnp.concatenate(
                [d_re, d_im], axis=0
            ).astype(BF16)
            return carry

        lax.fori_loop(0, GL, lower, 0, unroll=4)

    def far_part(offset):
        first = block_of(offset) * LEAF
        rows = down[pl.ds(first, LEAF)].reshape(LEAF * COMPS, KD)
        res = dot(rows, w[...], NN_DIMS).astype(BF16)
        part[pl.ds(first, LEAF)] = res.reshape(LEAF, COMPS, KL)

    def far_src(way, step, i):
        offset = (4 - step) if way == 0 else (step - 4)
        return block_of(offset) * LEAF + i

    def far_first(way, step, i):
        return step == 0 or (step == 1 and (i < 2) == (way == 1))

    def far_has(way, step, i):
        return step > 0 or (i < 2) == (way == 0)

    def far_copy(way, step, i):
        if far_first(way, step, i):
            src = part.at[far_src(way, step, i)]
        else:
            src = (st_r if way == 0 else st_l).at[step, i]
        dst = (rs_r if way == 0 else rs_l).at[step, i]
        return remote(
            src, dst, rs_send.at[way, step, i], rs_recv.at[way, step, i], (right, left)[way]
        )

    fars = {
        (way, step, i): far_copy(way, step, i)
        for step in range(4)
        for i in range(LEAF)
        for way in range(2)
        if far_has(way, step, i)
    }
    orders = ((0, 1, 2, 3), (2, 3, 0, 1))

    far_part(4)
    for k in range(LEAF):
        for way in range(2):
            if far_has(way, 0, orders[way][k]):
                fars[way, 0, orders[way][k]].start()
    for step in range(1, 4):
        far_part(4 - step)
        far_part(step - 4)
        if step == 1:
            for way in range(2):
                for i in range(LEAF):
                    if far_first(way, 1, i):
                        fars[way, 1, i].start()
        if step == 3:
            far_part(0)
        for k in range(LEAF):
            for way in range(2):
                i = orders[way][k]
                if far_first(way, step, i):
                    continue
                fars[way, step - 1, i].wait_recv()
                came = (rs_r if way == 0 else rs_l)[step - 1, i].astype(F32)
                mine = part[far_src(way, step, i)].astype(F32)
                (st_r if way == 0 else st_l)[step, i] = (came + mine).astype(BF16)
                fars[way, step, i].start()

    for i in range(LEAF):
        for way in range(2):
            fars[way, 3, i].wait_recv()
        far = (
            part[samp * LEAF + i].astype(F32)
            + rs_r[3, i].astype(F32)
            + rs_l[3, i].astype(F32)
        ).astype(BF16)
        cat = jnp.concatenate([rad[i, p, r] for p in range(2) for r in range(2)], axis=1)
        g = dot(far, cat, NN_DIMS)
        re = (
            g[0:4, 0:128] + g[8:12, 128:256] + g[4:8, 256:384] + g[12:16, 384:512]
        )
        im = (
            g[8:12, 0:128] - g[0:4, 128:256] + g[12:16, 256:384] - g[4:8, 384:512]
        )
        out_ref[i] = jnp.concatenate([re, im], axis=0) + nearacc[i]

    for copy in gathers.values():
        copy.wait_send()
    cur_up.wait_send()
    cur_dn.wait_send()
    for up, dn in halos:
        up.wait_send()
        dn.wait_send()
    for copy in fars.values():
        copy.wait_send()


def tables(near_src, leaf_parent, leaf_shift, interp_idx, top_src, top_disp):
    group = lax.axis_index("box")
    first_leaf = (group * SAMP + lax.axis_index("samp")) * LEAF
    parent = leaf_parent - group * TOP
    ids = jnp.arange(GL, dtype=jnp.int32)
    key = parent * GL + ids
    rank = jnp.sum((key[None, :] < key[:, None]).astype(jnp.int32), axis=1)
    at = rank[None, :] == ids[:, None]
    order = jnp.sum(jnp.where(at, ids[None, :], 0), axis=1)
    sorted_parent = jnp.sum(jnp.where(at, parent[None, :], 0), axis=1)
    before = jnp.sum(jnp.where(rank[None, :] == ids[:, None] - 1, parent[None, :] + 1, 0), axis=1) - 1
    cont = (before == sorted_parent).astype(jnp.int32)
    boxes = jnp.arange(TOP, dtype=jnp.int32)
    upto = jnp.sum((parent[None, :] <= boxes[:, None]).astype(jnp.int32), axis=1)
    has = jnp.any(parent[None, :] == boxes[:, None], axis=1).astype(jnp.int32)
    last = jnp.maximum(upto - 1, 0)
    return jnp.concatenate(
        [
            order,
            cont,
            last,
            has,
            leaf_shift,
            parent,
            (near_src - first_leaf + LEAF).reshape(-1),
            interp_idx.reshape(-1),
            (top_src - group * TOP + RIM).reshape(-1),
            top_disp.reshape(-1),
        ]
    ).astype(jnp.int32)


def per_device(
    currents,
    radiation,
    near_blocks,
    near_src,
    leaf_parent,
    leaf_shift,
    shift_table,
    interp_idx,
    interp_val,
    top_src,
    top_disp,
    trans_table,
):
    ints = tables(near_src, leaf_parent, leaf_shift, interp_idx, top_src, top_disp)
    boxes = lax.axis_size("box")
    any_spec = pl.BlockSpec(memory_space=pl.ANY)
    dma = pltpu.SemaphoreType.DMA
    vm = pltpu.VMEM
    return pl.pallas_call(
        functools.partial(kernel, boxes),
        out_shape=jax.ShapeDtypeStruct((LEAF, 2 * EXC, 128), F32),
        in_specs=[pl.BlockSpec(memory_space=pltpu.SMEM)] + [any_spec] * 6,
        out_specs=pl.BlockSpec(memory_space=pltpu.VMEM),
        scratch_shapes=[
            vm((3 * LEAF, 8, 128), BF16),
            vm((3 * LEAF, 8, 256), BF16),
            vm((LEAF, 2, 2, KL, 128), BF16),
            vm((LEAF, NEAR, 2, 128, 128), BF16),
            vm((NSHIFT, 2, KD), BF16),
            vm((8, 2, 128, 128), BF16),
            vm((NDISP, 2, KD), BF16),
            vm((KD, KL), BF16),
            vm((CH, NSHIFT, 2, HALF, KC), F32),
            vm((CH, NDISP, 2, HALF, KC), F32),
            vm((LEAF, COMPS, KL), BF16),
            vm((3, LEAF, COMPS, KL), BF16),
            vm((3, LEAF, COMPS, KL), BF16),
            vm((LEAF, COMPS, KL), BF16),
            vm((CH, GL, COMPS, KC), F32),
            vm((GL, COMPS, KC), F32),
            vm((CH, TOP, COMPS, KC), BF16),
            vm((CH, RIM, COMPS, KC), BF16),
            vm((CH, RIM, COMPS, KC), BF16),
            vm((CH, TOP + 2 * RIM, COMPS, KC), F32),
            vm((TOP, COMPS, KC), F32),
            vm((GL, COMPS, KD), BF16),
            vm((GL, COMPS, KL), BF16),
            vm((4, LEAF, COMPS, KL), BF16),
            vm((4, LEAF, COMPS, KL), BF16),
            vm((4, LEAF, COMPS, KL), BF16),
            vm((4, LEAF, COMPS, KL), BF16),
            vm((LEAF, 2 * EXC, 128), F32),
            dma((12,)),
            dma((4,)),
            dma((2, 4, LEAF)),
            dma((2, 4, LEAF)),
            dma((2, CH)),
            dma((2, CH)),
            dma((2, 4, LEAF)),
            dma((2, 4, LEAF)),
        ],
        compiler_params=pltpu.CompilerParams(collective_id=0, has_side_effects=True),
    )(ints, currents, radiation, near_blocks, shift_table, interp_val, trans_table)


def solution(mesh):
    placed = (
        P(("box", "samp"), None, None),
        P(("box", "samp"), None, None, None, None),
        P(("box", "samp"), None, None, None, None),
        P(("box", "samp"), None),
        P("box"),
        P("box"),
        P(None, None, "samp"),
        P("samp", None),
        P("samp", None, None, None),
        P("box", None),
        P("box", None),
        P(None, None, "samp"),
    )
    return jax.shard_map(
        per_device,
        mesh=mesh,
        in_specs=placed,
        out_specs=P(("box", "samp"), None, None),
        check_vma=False,
    )
```

```python
import functools

import jax
import jax.numpy as jnp
from jax import lax
from jax.experimental import pallas as pl
from jax.experimental.pallas import tpu as pltpu
from jax.sharding import PartitionSpec as P

MESH = pl.DeviceIdType.MESH
F32 = jnp.float32
BF16 = jnp.bfloat16
EXC = 4
COMPS = 16
HALF = 8
KL = 512
KD = 1024
BLK = 128
CH = 4
KC = KD // CH
LEAF = 4
SAMP = 8
GL = LEAF * SAMP
TOP = 16
RIM = 8
NEAR = 8
ILIST = 16
NDISP = 32
NSHIFT = 8

NT_DIMS = (((1,), (1,)), ((), ()))
NN_DIMS = (((1,), (0,)), ((), ()))


def dot(a, b, dims):
    return lax.dot_general(a, b, dims, preferred_element_type=F32)


def kernel(
    boxes,
    parent_hbm,
    turn_hbm,
    near_idx_hbm,
    interp_hbm,
    src_hbm,
    disp_hbm,
    cur_hbm,
    rad_hbm,
    near_hbm,
    shift_hbm,
    val_hbm,
    trans_hbm,
    out_ref,
    parent_s,
    turn_s,
    near_s,
    interp_s,
    src_s,
    disp_s,
    order_s,
    parent_v,
    order_v,
    nbr,
    xbuf,
    rad,
    near,
    shift_raw,
    val,
    trans_raw,
    w,
    sh,
    tr,
    own,
    ag,
    ag_f,
    shifted,
    seg,
    topbf,
    halo_l,
    halo_r,
    srcf,
    inc,
    down,
    part,
    near_in,
    relay_in,
    half_in,
    relay_out,
    end_in,
    nearacc,
    local_sem,
    cur_sem,
    ag_send,
    ag_recv,
    halo_send,
    halo_recv,
    rs_send,
    rs_recv,
):
    box = lax.axis_index("box")
    samp = lax.axis_index("samp")
    total = boxes * SAMP
    ones = [(box, lax.rem(samp + d, SAMP)) for d in (1, SAMP - 1)]
    twos = [(box, lax.rem(samp + d, SAMP)) for d in (2, SAMP - 2)]
    box_next = (lax.rem(box + 1, boxes), samp)
    box_prev = (lax.rem(box + boxes - 1, boxes), samp)
    flat = box * SAMP + samp
    flat_up = lax.rem(flat + 1, total)
    flat_dn = lax.rem(flat + total - 1, total)
    dev_up = (flat_up // SAMP, lax.rem(flat_up, SAMP))
    dev_dn = (flat_dn // SAMP, lax.rem(flat_dn, SAMP))

    def local(src, dst, index):
        return pltpu.make_async_copy(src, dst, local_sem.at[index])

    cur_copy = local(cur_hbm, nbr.at[pl.ds(LEAF, LEAF)], 0)
    rad_copies = [local(rad_hbm.at[i], rad.at[i], 1 + i) for i in range(LEAF)]
    val_copy = local(val_hbm, val, 5)
    shift_copy = local(shift_hbm, shift_raw, 6)
    trans_copy = local(trans_hbm, trans_raw, 7)
    near_copies = [local(near_hbm.at[i], near.at[i], 8 + i) for i in range(LEAF)]
    index_copies = [
        local(src, dst, 12 + k)
        for k, (src, dst) in enumerate(
            (
                (parent_hbm, parent_v),
                (interp_hbm, interp_s),
                (turn_hbm, turn_s),
                (near_idx_hbm, near_s),
                (parent_hbm, parent_s),
                (src_hbm, src_s),
                (disp_hbm, disp_s),
            )
        )
    ]
    order_copy = local(order_v, order_s, 19)
    cur_copy.start()
    for copy in rad_copies:
        copy.start()
    barrier = pltpu.get_barrier_semaphore()
    for dev in (*twos, *ones, box_next, box_prev, dev_up, dev_dn):
        pl.semaphore_signal(barrier, inc=1, device_id=dev, device_id_type=MESH)
    for copy in (val_copy, shift_copy, *index_copies, trans_copy, *near_copies):
        copy.start()

    def remote(src, dst, send, recv, dev):
        return pltpu.make_async_remote_copy(
            src_ref=src,
            dst_ref=dst,
            send_sem=send,
            recv_sem=recv,
            device_id=dev,
            device_id_type=MESH,
        )

    def half(h):
        return pl.ds(2 * h, 2)

    def gather_copy(way, dist, h):
        src = own.at[half(h)] if dist < 3 else ag.at[way, 1, half(h)]
        dst = ag_f.at[half(h)] if dist == 4 else ag.at[way, dist - 1, half(h)]
        dev = (ones if dist % 2 else twos)[way]
        return remote(
            src, dst, ag_send.at[way, dist - 1, h], ag_recv.at[way, dist - 1, h], dev
        )

    gathers = {
        (way, dist, h): gather_copy(way, dist, h)
        for dist in (1, 2, 3, 4)
        for h in range(2)
        for way in range(2)
        if dist < 4 or h == way
    }

    cur_copy.wait()
    for i in range(LEAF):
        x = nbr[LEAF + i].astype(F32)
        c_re, c_im = x[:EXC], x[EXC:]
        zero = jnp.zeros_like(c_re)
        lhs = jnp.concatenate(
            [
                jnp.concatenate([c_re, zero, c_im, zero], axis=0),
                jnp.concatenate([-c_im, zero, c_re, zero], axis=0),
                jnp.concatenate([zero, c_re, zero, c_im], axis=0),
                jnp.concatenate([zero, -c_im, zero, c_re], axis=0),
            ],
            axis=1,
        ).astype(BF16)
        rad_copies[i].wait()
        cat = jnp.concatenate([rad[i, p, r] for p in range(2) for r in range(2)], axis=1)
        own[i] = dot(lhs, cat, NT_DIMS).astype(BF16)
        if i == 1:
            pl.semaphore_wait(barrier, 8)
        if i % 2:
            for dist in (2, 1):
                for way in range(2):
                    gathers[way, dist, i // 2].start()

    cur_up = remote(cur_hbm, nbr.at[pl.ds(0, LEAF)], cur_sem.at[0], cur_sem.at[2], dev_up)
    cur_dn = remote(
        cur_hbm, nbr.at[pl.ds(2 * LEAF, LEAF)], cur_sem.at[1], cur_sem.at[3], dev_dn
    )
    cur_up.start()
    cur_dn.start()

    for copy in index_copies:
        copy.wait()
    order_leaves(parent_v[...] & (TOP - 1), order_v)
    order_copy.start()

    val_copy.wait()
    for b in range(KD // BLK):
        first = interp_s[0, b]
        second = interp_s[1, b]
        for q in range(KL // BLK):
            tile = jnp.where(
                first == q,
                val[b, 0],
                jnp.where(second == q, val[b, 1], jnp.zeros((BLK, BLK), BF16)),
            )
            w[pl.ds(b * BLK, BLK), pl.ds(q * BLK, BLK)] = tile
    shift_copy.wait()
    for n in range(NSHIFT):
        row = shift_raw[n].astype(F32)
        for c in range(CH):
            for r in range(2):
                sh[c, n, r] = jnp.broadcast_to(
                    row[r : r + 1, c * KC : (c + 1) * KC], (HALF, KC)
                )

    def lift(rows, first_leaf):
        for c in range(CH):
            moved = dot(rows, w[pl.ds(c * KC, KC), :], NT_DIMS)
            for i in range(LEAF):
                leaf = first_leaf + i
                turn = turn_s[leaf]
                s_re = sh[c, turn, 0]
                s_im = sh[c, turn, 1]
                m_re = moved[i * COMPS : i * COMPS + HALF]
                m_im = moved[i * COMPS + HALF : (i + 1) * COMPS]
                shifted[c, leaf, 0:HALF] = m_re * s_re - m_im * s_im
                shifted[c, leaf, HALF:COMPS] = m_re * s_im + m_im * s_re

    def rows_of(block):
        return block.reshape(LEAF * COMPS, KL)

    def block_of(offset):
        return lax.rem(samp + offset + SAMP, SAMP)

    lift(rows_of(own[...]), block_of(0) * LEAF)

    def near_leaf(i):
        near_copies[i].wait()
        acc = jnp.zeros((HALF, BLK), F32)
        for n in range(NEAR):
            lhs = xbuf[jnp.clip(near_s[i, n] - (flat - 1) * LEAF, 0, 3 * LEAF - 1)]
            acc += dot(lhs, jnp.concatenate([near[i, n, 0], near[i, n, 1]], axis=1), NT_DIMS)
        nearacc[i] = acc

    def expand_trans():
        trans_copy.wait()

        def body(n, carry):
            row = trans_raw[n].astype(F32)
            for c in range(CH):
                for r in range(2):
                    tr[c, n, r] = jnp.broadcast_to(
                        row[r : r + 1, c * KC : (c + 1) * KC], (HALF, KC)
                    )
            return carry

        lax.fori_loop(0, NDISP, body, 0)

    for h in range(2):
        for way in range(2):
            gathers[way, 2, h].wait_recv()
            if h == way:
                gathers[way, 4, h].start()
            gathers[way, 3, h].start()
    for dist in (2, 1, 3):
        for way in range(2):
            if dist != 2:
                gathers[way, dist, 0].wait_recv()
                gathers[way, dist, 1].wait_recv()
            lift(rows_of(ag[way, dist - 1]), block_of(dist if way else -dist) * LEAF)
    gathers[0, 4, 0].wait_recv()
    gathers[1, 4, 1].wait_recv()
    lift(rows_of(ag_f[...]), block_of(4) * LEAF)

    order_copy.wait()
    halos = []
    for c in range(CH):

        def sum_step(j, acc):
            keep = order_s[1, j]
            value = shifted[c, order_s[0, j]]
            acc = jnp.where(keep == 1, acc, jnp.zeros_like(acc)) + value
            seg[j] = acc
            return acc

        lax.fori_loop(0, GL, sum_step, jnp.zeros((COMPS, KC), F32), unroll=4)

        def top_step(t, carry):
            value = seg[order_s[2, t]]
            value = jnp.where(order_s[3, t] == 1, value, jnp.zeros_like(value)).astype(BF16)
            topbf[c, t] = value
            srcf[c, RIM + t] = value.astype(F32)
            return carry

        lax.fori_loop(0, TOP, top_step, 0, unroll=4)
        up = remote(
            topbf.at[c, pl.ds(TOP - RIM, RIM)],
            halo_l.at[c],
            halo_send.at[0, c],
            halo_recv.at[0, c],
            box_next,
        )
        dn = remote(
            topbf.at[c, pl.ds(0, RIM)],
            halo_r.at[c],
            halo_send.at[1, c],
            halo_recv.at[1, c],
            box_prev,
        )
        up.start()
        dn.start()
        halos.append((up, dn))
    expand_trans()

    for c in range(CH):
        halos[c][0].wait_recv()
        halos[c][1].wait_recv()

        def widen(t, carry):
            srcf[c, t] = halo_l[c, t].astype(F32)
            srcf[c, RIM + TOP + t] = halo_r[c, t].astype(F32)
            return carry

        lax.fori_loop(0, RIM, widen, 0, unroll=2)

        def move(t, carry):
            acc_re = jnp.zeros((HALF, KC), F32)
            acc_im = jnp.zeros((HALF, KC), F32)
            for j in range(ILIST):
                source = (src_s[t, j] - (box * TOP - RIM)) & (2 * TOP - 1)
                disp = disp_s[t, j]
                s_re = srcf[c, source, 0:HALF]
                s_im = srcf[c, source, HALF:COMPS]
                t_re = tr[c, disp, 0]
                t_im = tr[c, disp, 1]
                acc_re += t_re * s_re - t_im * s_im
                acc_im += t_re * s_im + t_im * s_re
            value = jnp.concatenate([acc_re, acc_im], axis=0)
            inc[t] = value.astype(BF16).astype(F32)
            return carry

        lax.fori_loop(0, TOP, move, 0)

        def lower(at, carry):
            leaf = lax.rem(at + samp * LEAF, GL)
            value = inc[parent_s[0, leaf] & (TOP - 1)]
            turn = turn_s[leaf]
            s_re = sh[c, turn, 0]
            s_im = sh[c, turn, 1]
            v_re, v_im = value[:HALF], value[HALF:]
            d_re = s_re * v_re + s_im * v_im
            d_im = s_re * v_im - s_im * v_re
            down[at, :, c * KC : (c + 1) * KC] = jnp.concatenate(
                [d_re, d_im], axis=0
            ).astype(BF16)
            return carry

        lax.fori_loop(0, GL, lower, 0, unroll=8)

    def far_part(first, count):
        rows = down[pl.ds(first * LEAF, count * LEAF)].reshape(count * LEAF * COMPS, KD)
        res = dot(rows, w[...], NN_DIMS).astype(BF16)
        part[pl.ds(first * LEAF, count * LEAF)] = res.reshape(count * LEAF, COMPS, KL)

    def part_half(offset, h):
        return pl.ds((offset % SAMP) * LEAF + 2 * h, 2)

    signs = (1, -1)
    relays = {}
    quarters = {}
    firsts = {}
    seconds = {}
    for way in range(2):
        quarters[way] = remote(
            part.at[part_half(4, way)],
            half_in.at[way],
            rs_send.at[way, 0, 0],
            rs_recv.at[way, 0, 0],
            twos[way],
        )
        firsts[way] = remote(
            part.at[pl.ds((signs[way] % SAMP) * LEAF, LEAF)],
            near_in.at[way],
            rs_send.at[way, 0, 1],
            rs_recv.at[way, 0, 1],
            ones[way],
        )
        for h in range(2):
            relays[way, h] = remote(
                part.at[part_half(3 * signs[way], h)],
                relay_in.at[way, half(h)],
                rs_send.at[way, 1, h],
                rs_recv.at[way, 1, h],
                ones[way],
            )
            seconds[way, h] = remote(
                relay_out.at[way, half(h)],
                end_in.at[way, half(h)],
                rs_send.at[way, 2, h],
                rs_recv.at[way, 2, h],
                twos[way],
            )

    far_part(3, 3)
    for way in range(2):
        quarters[way].start()
        relays[way, 1 - way].start()
    for way in range(2):
        relays[way, way].start()
    far_part(6, 2)
    far_part(1, 2)
    for way in range(2):
        firsts[way].start()
    far_part(0, 1)
    cur_up.wait_recv()
    cur_dn.wait_recv()
    for m in range(3 * LEAF):
        x = nbr[m].astype(F32)
        turned = jnp.concatenate([-x[EXC:], x[:EXC]], axis=0)
        xbuf[m] = jnp.concatenate([x, turned], axis=1).astype(BF16)
    near_leaf(0)
    for way in range(2):
        h = 1 - way
        relays[way, h].wait_recv()
        mine = part[part_half(2 * signs[way], h)].astype(F32)
        relay_out[way, half(h)] = (mine + relay_in[way, half(h)].astype(F32)).astype(BF16)
        seconds[way, h].start()
    for way in range(2):
        h = way
        relays[way, h].wait_recv()
        quarters[way].wait_recv()
        mine = part[part_half(2 * signs[way], h)].astype(F32)
        relay_out[way, half(h)] = (
            mine + relay_in[way, half(h)].astype(F32) + half_in[way].astype(F32)
        ).astype(BF16)
        seconds[way, h].start()
    near_leaf(1)
    near_leaf(2)
    near_leaf(3)
    for way in range(2):
        firsts[way].wait_recv()
    for way in range(2):
        seconds[way, 1 - way].wait_recv()
    for way in range(2):
        seconds[way, way].wait_recv()

    for i in range(LEAF):
        far = (
            part[i].astype(F32)
            + (near_in[0, i].astype(F32) + near_in[1, i].astype(F32))
            + (end_in[0, i].astype(F32) + end_in[1, i].astype(F32))
        ).astype(BF16)
        cat = jnp.concatenate([rad[i, p, r] for p in range(2) for r in range(2)], axis=1)
        g = dot(far, cat, NN_DIMS)
        re = (
            g[0:4, 0:128] + g[8:12, 128:256] + g[4:8, 256:384] + g[12:16, 384:512]
        )
        im = (
            g[8:12, 0:128] - g[0:4, 128:256] + g[12:16, 256:384] - g[4:8, 384:512]
        )
        out_ref[i] = jnp.concatenate([re, im], axis=0) + nearacc[i]

    for copy in gathers.values():
        copy.wait_send()
    cur_up.wait_send()
    cur_dn.wait_send()
    for up, dn in halos:
        up.wait_send()
        dn.wait_send()
    for group in (quarters, firsts, relays, seconds):
        for copy in group.values():
            copy.wait_send()


def order_leaves(row, table):
    wide = (GL, GL)
    ups = lax.broadcasted_iota(jnp.int32, wide, 0)
    ids = lax.broadcasted_iota(jnp.int32, wide, 1)
    row = jnp.broadcast_to(row, wide)
    col = jnp.sum(jnp.where(ups == ids, row, 0), axis=1, keepdims=True)
    col = jnp.broadcast_to(col, wide)
    lower = (row * GL + ids) < (col * GL + ups)
    rank = jnp.sum(lower.astype(jnp.int32), axis=1, keepdims=True)
    rank = jnp.broadcast_to(rank, wide)
    at = rank == ids

    def total(value):
        return jnp.sum(value, axis=0, keepdims=True)

    order = total(jnp.where(at, ups, 0))
    here = total(jnp.where(at, col, 0))
    before = total(jnp.where(rank == ids - 1, col + 1, 0)) - 1
    last = jnp.maximum(total((col <= ids).astype(jnp.int32)) - 1, 0)
    has = jnp.minimum(total((col == ids).astype(jnp.int32)), 1)
    table[...] = jnp.zeros_like(table)
    table[0:1, 0:GL] = order
    table[1:2, 0:GL] = (before == here).astype(jnp.int32)
    table[2:3, 0:GL] = last
    table[3:4, 0:GL] = has


def per_device(
    currents,
    radiation,
    near_blocks,
    near_src,
    leaf_parent,
    leaf_shift,
    shift_table,
    interp_idx,
    interp_val,
    top_src,
    top_disp,
    trans_table,
):
    boxes = lax.axis_size("box")
    any_spec = pl.BlockSpec(memory_space=pl.ANY)
    dma = pltpu.SemaphoreType.DMA
    vm = pltpu.VMEM
    sm = pltpu.SMEM
    i32 = jnp.int32
    return pl.pallas_call(
        functools.partial(kernel, boxes),
        out_shape=jax.ShapeDtypeStruct((LEAF, 2 * EXC, 128), F32),
        in_specs=[any_spec] * 12,
        out_specs=pl.BlockSpec(memory_space=pltpu.VMEM),
        scratch_shapes=[
            sm((1, GL), i32),
            sm((GL,), i32),
            sm((LEAF, NEAR), i32),
            sm((2, 8), i32),
            sm((TOP, ILIST), i32),
            sm((TOP, ILIST), i32),
            sm((8, 128), i32),
            vm((1, GL), i32),
            vm((8, 128), i32),
            vm((3 * LEAF, 8, 128), BF16),
            vm((3 * LEAF, 8, 256), BF16),
            vm((LEAF, 2, 2, KL, 128), BF16),
            vm((LEAF, NEAR, 2, 128, 128), BF16),
            vm((NSHIFT, 2, KD), BF16),
            vm((8, 2, 128, 128), BF16),
            vm((NDISP, 2, KD), BF16),
            vm((KD, KL), BF16),
            vm((CH, NSHIFT, 2, HALF, KC), F32),
            vm((CH, NDISP, 2, HALF, KC), F32),
            vm((LEAF, COMPS, KL), BF16),
            vm((2, 3, LEAF, COMPS, KL), BF16),
            vm((LEAF, COMPS, KL), BF16),
            vm((CH, GL, COMPS, KC), F32),
            vm((GL, COMPS, KC), F32),
            vm((CH, TOP, COMPS, KC), BF16),
            vm((CH, RIM, COMPS, KC), BF16),
            vm((CH, RIM, COMPS, KC), BF16),
            vm((CH, TOP + 2 * RIM, COMPS, KC), F32),
            vm((TOP, COMPS, KC), F32),
            vm((GL, COMPS, KD), BF16),
            vm((GL, COMPS, KL), BF16),
            vm((2, LEAF, COMPS, KL), BF16),
            vm((2, LEAF, COMPS, KL), BF16),
            vm((2, 2, COMPS, KL), BF16),
            vm((2, LEAF, COMPS, KL), BF16),
            vm((2, LEAF, COMPS, KL), BF16),
            vm((LEAF, 2 * EXC, 128), F32),
            dma((20,)),
            dma((4,)),
            dma((2, 4, 2)),
            dma((2, 4, 2)),
            dma((2, CH)),
            dma((2, CH)),
            dma((2, 3, 2)),
            dma((2, 3, 2)),
        ],
        compiler_params=pltpu.CompilerParams(collective_id=0, has_side_effects=True),
    )(leaf_parent.reshape(1, GL), leaf_shift, near_src, interp_idx.T, top_src, top_disp, currents, radiation, near_blocks, shift_table, interp_val, trans_table)


def solution(mesh):
    placed = (
        P(("box", "samp"), None, None),
        P(("box", "samp"), None, None, None, None),
        P(("box", "samp"), None, None, None, None),
        P(("box", "samp"), None),
        P("box"),
        P("box"),
        P(None, None, "samp"),
        P("samp", None),
        P("samp", None, None, None),
        P("box", None),
        P("box", None),
        P(None, None, "samp"),
    )
    return jax.shard_map(
        per_device,
        mesh=mesh,
        in_specs=placed,
        out_specs=P(("box", "samp"), None, None),
        check_vma=False,
    )
```

```python
import functools

import jax
import jax.numpy as jnp
from jax import lax
from jax.experimental import pallas as pl
from jax.experimental.pallas import tpu as pltpu
from jax.sharding import PartitionSpec as P

MESH = pl.DeviceIdType.MESH
F32 = jnp.float32
BF16 = jnp.bfloat16
EXC = 4
COMPS = 16
HALF = 8
KL = 512
KD = 1024
BLK = 128
CH = 4
KC = KD // CH
LEAF = 4
SAMP = 8
GL = LEAF * SAMP
TOP = 16
RIM = 8
NEAR = 8
ILIST = 16
NDISP = 32
NSHIFT = 8

NT_DIMS = (((1,), (1,)), ((), ()))
NN_DIMS = (((1,), (0,)), ((), ()))


def dot(a, b, dims):
    return lax.dot_general(a, b, dims, preferred_element_type=F32)


def kernel(
    boxes,
    parent_hbm,
    turn_hbm,
    near_idx_hbm,
    interp_hbm,
    src_hbm,
    disp_hbm,
    cur_hbm,
    rad_hbm,
    near_hbm,
    shift_hbm,
    val_hbm,
    trans_hbm,
    out_ref,
    parent_s,
    turn_s,
    near_s,
    interp_s,
    src_s,
    disp_s,
    order_s,
    parent_v,
    order_v,
    nbr,
    xbuf,
    rad,
    near,
    shift_raw,
    val,
    trans_raw,
    w,
    sh,
    tr,
    own,
    ag,
    ag_f,
    shifted,
    seg,
    topbf,
    halo_l,
    halo_r,
    srcf,
    inc,
    down,
    part,
    near_in,
    relay_in,
    half_in,
    relay_out,
    end_in,
    nearacc,
    local_sem,
    cur_sem,
    ag_send,
    ag_recv,
    halo_send,
    halo_recv,
    rs_send,
    rs_recv,
):
    box = lax.axis_index("box")
    samp = lax.axis_index("samp")
    total = boxes * SAMP
    ones = [(box, lax.rem(samp + d, SAMP)) for d in (1, SAMP - 1)]
    twos = [(box, lax.rem(samp + d, SAMP)) for d in (2, SAMP - 2)]
    box_next = (lax.rem(box + 1, boxes), samp)
    box_prev = (lax.rem(box + boxes - 1, boxes), samp)
    flat = box * SAMP + samp
    flat_up = lax.rem(flat + 1, total)
    flat_dn = lax.rem(flat + total - 1, total)
    dev_up = (flat_up // SAMP, lax.rem(flat_up, SAMP))
    dev_dn = (flat_dn // SAMP, lax.rem(flat_dn, SAMP))

    def local(src, dst, index):
        return pltpu.make_async_copy(src, dst, local_sem.at[index])

    cur_copy = local(cur_hbm, nbr.at[pl.ds(LEAF, LEAF)], 0)
    rad_copies = [local(rad_hbm.at[i], rad.at[i], 1 + i) for i in range(LEAF)]
    val_copy = local(val_hbm, val, 5)
    shift_copy = local(shift_hbm, shift_raw, 6)
    trans_copy = local(trans_hbm, trans_raw, 7)
    near_copies = [local(near_hbm.at[i], near.at[i], 8 + i) for i in range(LEAF)]
    index_copies = [
        local(src, dst, 12 + k)
        for k, (src, dst) in enumerate(
            (
                (parent_hbm, parent_v),
                (interp_hbm, interp_s),
                (turn_hbm, turn_s),
                (near_idx_hbm, near_s),
                (parent_hbm, parent_s),
                (src_hbm, src_s),
                (disp_hbm, disp_s),
            )
        )
    ]
    order_copy = local(order_v, order_s, 19)
    cur_copy.start()
    for copy in rad_copies:
        copy.start()
    barrier = pltpu.get_barrier_semaphore()
    for dev in (*twos, *ones, box_next, box_prev, dev_up, dev_dn):
        pl.semaphore_signal(barrier, inc=1, device_id=dev, device_id_type=MESH)
    for copy in (val_copy, shift_copy, *index_copies, trans_copy, *near_copies):
        copy.start()

    def remote(src, dst, send, recv, dev):
        return pltpu.make_async_remote_copy(
            src_ref=src,
            dst_ref=dst,
            send_sem=send,
            recv_sem=recv,
            device_id=dev,
            device_id_type=MESH,
        )

    def half(h):
        return pl.ds(2 * h, 2)

    def gather_copy(way, dist, h):
        src = own.at[half(h)] if dist < 3 else ag.at[way, 1, half(h)]
        dst = ag_f.at[half(h)] if dist == 4 else ag.at[way, dist - 1, half(h)]
        dev = (ones if dist % 2 else twos)[way]
        return remote(
            src, dst, ag_send.at[way, dist - 1, h], ag_recv.at[way, dist - 1, h], dev
        )

    gathers = {
        (way, dist, h): gather_copy(way, dist, h)
        for dist in (1, 2, 3, 4)
        for h in range(2)
        for way in range(2)
        if dist < 4 or h == way
    }

    cur_copy.wait()
    for i in range(LEAF):
        x = nbr[LEAF + i].astype(F32)
        c_re, c_im = x[:EXC], x[EXC:]
        zero = jnp.zeros_like(c_re)
        lhs = jnp.concatenate(
            [
                jnp.concatenate([c_re, zero, c_im, zero], axis=0),
                jnp.concatenate([-c_im, zero, c_re, zero], axis=0),
                jnp.concatenate([zero, c_re, zero, c_im], axis=0),
                jnp.concatenate([zero, -c_im, zero, c_re], axis=0),
            ],
            axis=1,
        ).astype(BF16)
        rad_copies[i].wait()
        cat = jnp.concatenate([rad[i, p, r] for p in range(2) for r in range(2)], axis=1)
        own[i] = dot(lhs, cat, NT_DIMS).astype(BF16)
        if i == 1:
            pl.semaphore_wait(barrier, 8)
        if i % 2:
            for way in range(2):
                gathers[way, 2, i // 2].start()
    for h in range(2):
        for way in range(2):
            gathers[way, 1, h].start()

    cur_up = remote(cur_hbm, nbr.at[pl.ds(0, LEAF)], cur_sem.at[0], cur_sem.at[2], dev_up)
    cur_dn = remote(
        cur_hbm, nbr.at[pl.ds(2 * LEAF, LEAF)], cur_sem.at[1], cur_sem.at[3], dev_dn
    )
    cur_up.start()
    cur_dn.start()

    for copy in index_copies:
        copy.wait()
    order_leaves(parent_v[...] & (TOP - 1), order_v)
    order_copy.start()

    val_copy.wait()
    for b in range(KD // BLK):
        first = interp_s[0, b]
        second = interp_s[1, b]
        for q in range(KL // BLK):
            tile = jnp.where(
                first == q,
                val[b, 0],
                jnp.where(second == q, val[b, 1], jnp.zeros((BLK, BLK), BF16)),
            )
            w[pl.ds(b * BLK, BLK), pl.ds(q * BLK, BLK)] = tile
    shift_copy.wait()
    for n in range(NSHIFT):
        row = shift_raw[n].astype(F32)
        for c in range(CH):
            for r in range(2):
                sh[c, n, r] = jnp.broadcast_to(
                    row[r : r + 1, c * KC : (c + 1) * KC], (HALF, KC)
                )

    def lift(rows, first_leaf, chunks=range(CH)):
        for c in chunks:
            moved = dot(rows, w[pl.ds(c * KC, KC), :], NT_DIMS)
            for i in range(LEAF):
                leaf = first_leaf + i
                turn = turn_s[leaf]
                s_re = sh[c, turn, 0]
                s_im = sh[c, turn, 1]
                m_re = moved[i * COMPS : i * COMPS + HALF]
                m_im = moved[i * COMPS + HALF : (i + 1) * COMPS]
                shifted[c, leaf, 0:HALF] = m_re * s_re - m_im * s_im
                shifted[c, leaf, HALF:COMPS] = m_re * s_im + m_im * s_re

    def rows_of(block):
        return block.reshape(LEAF * COMPS, KL)

    def block_of(offset):
        return lax.rem(samp + offset + SAMP, SAMP)

    lift(rows_of(own[...]), block_of(0) * LEAF)

    def near_leaf(i):
        near_copies[i].wait()
        acc = jnp.zeros((HALF, BLK), F32)
        for n in range(NEAR):
            lhs = xbuf[jnp.clip(near_s[i, n] - (flat - 1) * LEAF, 0, 3 * LEAF - 1)]
            acc += dot(lhs, jnp.concatenate([near[i, n, 0], near[i, n, 1]], axis=1), NT_DIMS)
        nearacc[i] = acc

    def expand_trans():
        trans_copy.wait()

        def body(n, carry):
            row = trans_raw[n].astype(F32)
            for c in range(CH):
                for r in range(2):
                    tr[c, n, r] = jnp.broadcast_to(
                        row[r : r + 1, c * KC : (c + 1) * KC], (HALF, KC)
                    )
            return carry

        lax.fori_loop(0, NDISP, body, 0)

    for h in range(2):
        for way in range(2):
            gathers[way, 2, h].wait_recv()
            if h == way:
                gathers[way, 4, h].start()
            gathers[way, 3, h].start()
    for dist in (2, 1, 3):
        for way in range(2):
            if dist != 2:
                gathers[way, dist, 0].wait_recv()
                gathers[way, dist, 1].wait_recv()
            lift(rows_of(ag[way, dist - 1]), block_of(dist if way else -dist) * LEAF)
    gathers[0, 4, 0].wait_recv()
    gathers[1, 4, 1].wait_recv()
    order_copy.wait()
    halos = []
    for c in range(CH):
        lift(rows_of(ag_f[...]), block_of(4) * LEAF, (c,))

        def sum_step(j, acc):
            keep = order_s[1, j]
            value = shifted[c, order_s[0, j]]
            acc = jnp.where(keep == 1, acc, jnp.zeros_like(acc)) + value
            seg[j] = acc
            return acc

        lax.fori_loop(0, GL, sum_step, jnp.zeros((COMPS, KC), F32), unroll=16)

        def top_step(t, carry):
            value = seg[order_s[2, t]]
            value = jnp.where(order_s[3, t] == 1, value, jnp.zeros_like(value)).astype(BF16)
            topbf[c, t] = value
            srcf[c, RIM + t] = value.astype(F32)
            return carry

        lax.fori_loop(0, TOP, top_step, 0, unroll=16)
        up = remote(
            topbf.at[c, pl.ds(TOP - RIM, RIM)],
            halo_l.at[c],
            halo_send.at[0, c],
            halo_recv.at[0, c],
            box_next,
        )
        dn = remote(
            topbf.at[c, pl.ds(0, RIM)],
            halo_r.at[c],
            halo_send.at[1, c],
            halo_recv.at[1, c],
            box_prev,
        )
        up.start()
        dn.start()
        halos.append((up, dn))
    expand_trans()

    for c in range(CH):
        halos[c][0].wait_recv()
        halos[c][1].wait_recv()

        def widen(t, carry):
            srcf[c, t] = halo_l[c, t].astype(F32)
            srcf[c, RIM + TOP + t] = halo_r[c, t].astype(F32)
            return carry

        lax.fori_loop(0, RIM, widen, 0, unroll=2)

        def move(t, carry):
            acc_re = jnp.zeros((HALF, KC), F32)
            acc_im = jnp.zeros((HALF, KC), F32)
            for j in range(ILIST):
                source = (src_s[t, j] - (box * TOP - RIM)) & (2 * TOP - 1)
                disp = disp_s[t, j]
                s_re = srcf[c, source, 0:HALF]
                s_im = srcf[c, source, HALF:COMPS]
                t_re = tr[c, disp, 0]
                t_im = tr[c, disp, 1]
                acc_re += t_re * s_re - t_im * s_im
                acc_im += t_re * s_im + t_im * s_re
            value = jnp.concatenate([acc_re, acc_im], axis=0)
            inc[t] = value.astype(BF16).astype(F32)
            return carry

        lax.fori_loop(0, TOP, move, 0, unroll=2)

        def lower(at, carry):
            leaf = lax.rem(at + samp * LEAF, GL)
            value = inc[parent_s[0, leaf] & (TOP - 1)]
            turn = turn_s[leaf]
            s_re = sh[c, turn, 0]
            s_im = sh[c, turn, 1]
            v_re, v_im = value[:HALF], value[HALF:]
            d_re = s_re * v_re + s_im * v_im
            d_im = s_re * v_im - s_im * v_re
            down[at, :, c * KC : (c + 1) * KC] = jnp.concatenate(
                [d_re, d_im], axis=0
            ).astype(BF16)
            return carry

        lax.fori_loop(0, GL, lower, 0, unroll=16)

    def far_part(first, count):
        rows = down[pl.ds(first * LEAF, count * LEAF)].reshape(count * LEAF * COMPS, KD)
        res = dot(rows, w[...], NN_DIMS).astype(BF16)
        part[pl.ds(first * LEAF, count * LEAF)] = res.reshape(count * LEAF, COMPS, KL)

    def part_half(offset, h):
        return pl.ds((offset % SAMP) * LEAF + 2 * h, 2)

    signs = (1, -1)
    relays = {}
    quarters = {}
    firsts = {}
    seconds = {}
    for way in range(2):
        quarters[way] = remote(
            part.at[part_half(4, way)],
            half_in.at[way],
            rs_send.at[way, 0, 0],
            rs_recv.at[way, 0, 0],
            twos[way],
        )
        firsts[way] = remote(
            part.at[pl.ds((signs[way] % SAMP) * LEAF, LEAF)],
            near_in.at[way],
            rs_send.at[way, 0, 1],
            rs_recv.at[way, 0, 1],
            ones[way],
        )
        for h in range(2):
            relays[way, h] = remote(
                part.at[part_half(3 * signs[way], h)],
                relay_in.at[way, half(h)],
                rs_send.at[way, 1, h],
                rs_recv.at[way, 1, h],
                ones[way],
            )
            seconds[way, h] = remote(
                relay_out.at[way, half(h)],
                end_in.at[way, half(h)],
                rs_send.at[way, 2, h],
                rs_recv.at[way, 2, h],
                twos[way],
            )

    far_part(3, 3)
    for way in range(2):
        quarters[way].start()
        relays[way, 1 - way].start()
    for way in range(2):
        relays[way, way].start()
    far_part(6, 2)
    far_part(1, 2)
    for way in range(2):
        firsts[way].start()
    far_part(0, 1)
    cur_up.wait_recv()
    cur_dn.wait_recv()
    for m in range(3 * LEAF):
        x = nbr[m].astype(F32)
        turned = jnp.concatenate([-x[EXC:], x[:EXC]], axis=0)
        xbuf[m] = jnp.concatenate([x, turned], axis=1).astype(BF16)
    near_leaf(0)
    for way in range(2):
        h = 1 - way
        relays[way, h].wait_recv()
        mine = part[part_half(2 * signs[way], h)].astype(F32)
        relay_out[way, half(h)] = (mine + relay_in[way, half(h)].astype(F32)).astype(BF16)
        seconds[way, h].start()
    for way in range(2):
        h = way
        relays[way, h].wait_recv()
        quarters[way].wait_recv()
        mine = part[part_half(2 * signs[way], h)].astype(F32)
        relay_out[way, half(h)] = (
            mine + relay_in[way, half(h)].astype(F32) + half_in[way].astype(F32)
        ).astype(BF16)
        seconds[way, h].start()
    near_leaf(1)
    near_leaf(2)
    near_leaf(3)
    for way in range(2):
        firsts[way].wait_recv()
    for way in range(2):
        seconds[way, 1 - way].wait_recv()
    for way in range(2):
        seconds[way, way].wait_recv()

    for i in range(LEAF):
        far = (
            part[i].astype(F32)
            + (near_in[0, i].astype(F32) + near_in[1, i].astype(F32))
            + (end_in[0, i].astype(F32) + end_in[1, i].astype(F32))
        ).astype(BF16)
        cat = jnp.concatenate([rad[i, p, r] for p in range(2) for r in range(2)], axis=1)
        g = dot(far, cat, NN_DIMS)
        re = (
            g[0:4, 0:128] + g[8:12, 128:256] + g[4:8, 256:384] + g[12:16, 384:512]
        )
        im = (
            g[8:12, 0:128] - g[0:4, 128:256] + g[12:16, 256:384] - g[4:8, 384:512]
        )
        out_ref[i] = jnp.concatenate([re, im], axis=0) + nearacc[i]

    for copy in gathers.values():
        copy.wait_send()
    cur_up.wait_send()
    cur_dn.wait_send()
    for up, dn in halos:
        up.wait_send()
        dn.wait_send()
    for group in (quarters, firsts, relays, seconds):
        for copy in group.values():
            copy.wait_send()


def order_leaves(row, table):
    wide = (GL, GL)
    ups = lax.broadcasted_iota(jnp.int32, wide, 0)
    ids = lax.broadcasted_iota(jnp.int32, wide, 1)
    row = jnp.broadcast_to(row, wide)
    col = jnp.sum(jnp.where(ups == ids, row, 0), axis=1, keepdims=True)
    col = jnp.broadcast_to(col, wide)
    lower = (row * GL + ids) < (col * GL + ups)
    rank = jnp.sum(lower.astype(jnp.int32), axis=1, keepdims=True)
    rank = jnp.broadcast_to(rank, wide)
    at = rank == ids

    def total(value):
        return jnp.sum(value, axis=0, keepdims=True)

    order = total(jnp.where(at, ups, 0))
    here = total(jnp.where(at, col, 0))
    before = total(jnp.where(rank == ids - 1, col + 1, 0)) - 1
    last = jnp.maximum(total((col <= ids).astype(jnp.int32)) - 1, 0)
    has = jnp.minimum(total((col == ids).astype(jnp.int32)), 1)
    table[...] = jnp.zeros_like(table)
    table[0:1, 0:GL] = order
    table[1:2, 0:GL] = (before == here).astype(jnp.int32)
    table[2:3, 0:GL] = last
    table[3:4, 0:GL] = has


def per_device(
    currents,
    radiation,
    near_blocks,
    near_src,
    leaf_parent,
    leaf_shift,
    shift_table,
    interp_idx,
    interp_val,
    top_src,
    top_disp,
    trans_table,
):
    boxes = lax.axis_size("box")
    any_spec = pl.BlockSpec(memory_space=pl.ANY)
    dma = pltpu.SemaphoreType.DMA
    vm = pltpu.VMEM
    sm = pltpu.SMEM
    i32 = jnp.int32
    return pl.pallas_call(
        functools.partial(kernel, boxes),
        out_shape=pltpu.VMEM((LEAF, 2 * EXC, 128), F32),
        in_specs=[any_spec] * 12,
        out_specs=pl.BlockSpec(memory_space=pltpu.VMEM),
        scratch_shapes=[
            sm((1, GL), i32),
            sm((GL,), i32),
            sm((LEAF, NEAR), i32),
            sm((2, 8), i32),
            sm((TOP, ILIST), i32),
            sm((TOP, ILIST), i32),
            sm((8, 128), i32),
            vm((1, GL), i32),
            vm((8, 128), i32),
            vm((3 * LEAF, 8, 128), BF16),
            vm((3 * LEAF, 8, 256), BF16),
            vm((LEAF, 2, 2, KL, 128), BF16),
            vm((LEAF, NEAR, 2, 128, 128), BF16),
            vm((NSHIFT, 2, KD), BF16),
            vm((8, 2, 128, 128), BF16),
            vm((NDISP, 2, KD), BF16),
            vm((KD, KL), BF16),
            vm((CH, NSHIFT, 2, HALF, KC), F32),
            vm((CH, NDISP, 2, HALF, KC), F32),
            vm((LEAF, COMPS, KL), BF16),
            vm((2, 3, LEAF, COMPS, KL), BF16),
            vm((LEAF, COMPS, KL), BF16),
            vm((CH, GL, COMPS, KC), F32),
            vm((GL, COMPS, KC), F32),
            vm((CH, TOP, COMPS, KC), BF16),
            vm((CH, RIM, COMPS, KC), BF16),
            vm((CH, RIM, COMPS, KC), BF16),
            vm((CH, TOP + 2 * RIM, COMPS, KC), F32),
            vm((TOP, COMPS, KC), F32),
            vm((GL, COMPS, KD), BF16),
            vm((GL, COMPS, KL), BF16),
            vm((2, LEAF, COMPS, KL), BF16),
            vm((2, LEAF, COMPS, KL), BF16),
            vm((2, 2, COMPS, KL), BF16),
            vm((2, LEAF, COMPS, KL), BF16),
            vm((2, LEAF, COMPS, KL), BF16),
            vm((LEAF, 2 * EXC, 128), F32),
            dma((20,)),
            dma((4,)),
            dma((2, 4, 2)),
            dma((2, 4, 2)),
            dma((2, CH)),
            dma((2, CH)),
            dma((2, 3, 2)),
            dma((2, 3, 2)),
        ],
        compiler_params=pltpu.CompilerParams(collective_id=0, has_side_effects=True),
    )(leaf_parent.reshape(1, GL), leaf_shift, near_src, interp_idx.T, top_src, top_disp, currents, radiation, near_blocks, shift_table, interp_val, trans_table)


def solution(mesh):
    placed = (
        P(("box", "samp"), None, None),
        P(("box", "samp"), None, None, None, None),
        P(("box", "samp"), None, None, None, None),
        P(("box", "samp"), None),
        P("box"),
        P("box"),
        P(None, None, "samp"),
        P("samp", None),
        P("samp", None, None, None),
        P("box", None),
        P("box", None),
        P(None, None, "samp"),
    )
    return jax.shard_map(
        per_device,
        mesh=mesh,
        in_specs=placed,
        out_specs=P(("box", "samp"), None, None),
        check_vma=False,
    )
```

```python
import functools

import jax
import jax.numpy as jnp
from jax import lax
from jax.experimental import pallas as pl
from jax.experimental.pallas import tpu as pltpu
from jax.sharding import PartitionSpec as P

MESH = pl.DeviceIdType.MESH
F32 = jnp.float32
BF16 = jnp.bfloat16
EXC = 4
COMPS = 16
HALF = 8
KL = 512
KD = 1024
BLK = 128
CH = 4
KC = KD // CH
LEAF = 4
SAMP = 8
GL = LEAF * SAMP
TOP = 16
RIM = 8
NEAR = 8
ILIST = 16
NDISP = 32
NSHIFT = 8

NT_DIMS = (((1,), (1,)), ((), ()))
NN_DIMS = (((1,), (0,)), ((), ()))


def dot(a, b, dims):
    return lax.dot_general(a, b, dims, preferred_element_type=F32)


def kernel(
    boxes,
    parent_hbm,
    turn_hbm,
    near_idx_hbm,
    interp_hbm,
    src_hbm,
    disp_hbm,
    cur_hbm,
    rad_hbm,
    near_hbm,
    shift_hbm,
    val_hbm,
    trans_hbm,
    out_ref,
    parent_s,
    turn_s,
    near_s,
    interp_s,
    src_s,
    disp_s,
    order_s,
    parent_v,
    order_v,
    nbr,
    xbuf,
    rad,
    near,
    shift_raw,
    val,
    trans_raw,
    w,
    sh,
    tr,
    own,
    ag,
    ag_f,
    shifted,
    seg,
    topbf,
    halo_l,
    halo_r,
    srcf,
    inc,
    down,
    part,
    near_in,
    relay_in,
    half_in,
    relay_out,
    end_in,
    nearacc,
    local_sem,
    cur_sem,
    ag_send,
    ag_recv,
    halo_send,
    halo_recv,
    rs_send,
    rs_recv,
):
    box = lax.axis_index("box")
    samp = lax.axis_index("samp")
    total = boxes * SAMP
    ones = [(box, lax.rem(samp + d, SAMP)) for d in (1, SAMP - 1)]
    twos = [(box, lax.rem(samp + d, SAMP)) for d in (2, SAMP - 2)]
    box_next = (lax.rem(box + 1, boxes), samp)
    box_prev = (lax.rem(box + boxes - 1, boxes), samp)
    flat = box * SAMP + samp
    flat_up = lax.rem(flat + 1, total)
    flat_dn = lax.rem(flat + total - 1, total)
    dev_up = (flat_up // SAMP, lax.rem(flat_up, SAMP))
    dev_dn = (flat_dn // SAMP, lax.rem(flat_dn, SAMP))

    def local(src, dst, index):
        return pltpu.make_async_copy(src, dst, local_sem.at[index])

    cur_copy = local(cur_hbm, nbr.at[pl.ds(LEAF, LEAF)], 0)
    rad_copies = [local(rad_hbm.at[i], rad.at[i], 1 + i) for i in range(LEAF)]
    val_copy = local(val_hbm, val, 5)
    shift_copy = local(shift_hbm, shift_raw, 6)
    trans_copy = local(trans_hbm, trans_raw, 7)
    near_copies = [local(near_hbm.at[i], near.at[i], 8 + i) for i in range(LEAF)]
    index_copies = [
        local(src, dst, 12 + k)
        for k, (src, dst) in enumerate(
            (
                (parent_hbm, parent_v),
                (interp_hbm, interp_s),
                (turn_hbm, turn_s),
                (near_idx_hbm, near_s),
                (parent_hbm, parent_s),
                (src_hbm, src_s),
                (disp_hbm, disp_s),
            )
        )
    ]
    order_copy = local(order_v, order_s, 19)
    cur_copy.start()
    for copy in rad_copies:
        copy.start()
    barrier = pltpu.get_barrier_semaphore()
    for dev in (*twos, *ones, box_next, box_prev, dev_up, dev_dn):
        pl.semaphore_signal(barrier, inc=1, device_id=dev, device_id_type=MESH)
    for copy in (val_copy, shift_copy, *index_copies, trans_copy, *near_copies):
        copy.start()

    def remote(src, dst, send, recv, dev):
        return pltpu.make_async_remote_copy(
            src_ref=src,
            dst_ref=dst,
            send_sem=send,
            recv_sem=recv,
            device_id=dev,
            device_id_type=MESH,
        )

    def half(h):
        return pl.ds(2 * h, 2)

    def gather_copy(way, dist, h):
        src = own.at[half(h)] if dist < 3 else ag.at[way, 1, half(h)]
        dst = ag_f.at[half(h)] if dist == 4 else ag.at[way, dist - 1, half(h)]
        dev = (ones if dist % 2 else twos)[way]
        return remote(
            src, dst, ag_send.at[way, dist - 1, h], ag_recv.at[way, dist - 1, h], dev
        )

    gathers = {
        (way, dist, h): gather_copy(way, dist, h)
        for dist in (1, 2, 3, 4)
        for h in range(2)
        for way in range(2)
        if dist in (2, 3) or (dist == 4 and h == way)
    }
    for way in range(2):
        gathers[way, 1, 0] = remote(
            own, ag.at[way, 0], ag_send.at[way, 0, 0], ag_recv.at[way, 0, 0], ones[way]
        )

    cur_copy.wait()
    for i in range(LEAF):
        x = nbr[LEAF + i].astype(F32)
        c_re, c_im = x[:EXC], x[EXC:]
        zero = jnp.zeros_like(c_re)
        lhs = jnp.concatenate(
            [
                jnp.concatenate([c_re, zero, c_im, zero], axis=0),
                jnp.concatenate([-c_im, zero, c_re, zero], axis=0),
                jnp.concatenate([zero, c_re, zero, c_im], axis=0),
                jnp.concatenate([zero, -c_im, zero, c_re], axis=0),
            ],
            axis=1,
        ).astype(BF16)
        rad_copies[i].wait()
        cat = jnp.concatenate([rad[i, p, r] for p in range(2) for r in range(2)], axis=1)
        own[i] = dot(lhs, cat, NT_DIMS).astype(BF16)
        if i == 1:
            pl.semaphore_wait(barrier, 8)
        if i % 2:
            for way in range(2):
                gathers[way, 2, i // 2].start()
    for way in range(2):
        gathers[way, 1, 0].start()

    cur_up = remote(cur_hbm, nbr.at[pl.ds(0, LEAF)], cur_sem.at[0], cur_sem.at[2], dev_up)
    cur_dn = remote(
        cur_hbm, nbr.at[pl.ds(2 * LEAF, LEAF)], cur_sem.at[1], cur_sem.at[3], dev_dn
    )
    cur_up.start()
    cur_dn.start()

    for copy in index_copies:
        copy.wait()
    order_leaves(parent_v[...] & (TOP - 1), order_v)
    order_copy.start()

    val_copy.wait()
    for b in range(KD // BLK):
        first = interp_s[0, b]
        second = interp_s[1, b]
        for q in range(KL // BLK):
            tile = jnp.where(
                first == q,
                val[b, 0],
                jnp.where(second == q, val[b, 1], jnp.zeros((BLK, BLK), BF16)),
            )
            w[pl.ds(b * BLK, BLK), pl.ds(q * BLK, BLK)] = tile
    shift_copy.wait()
    for n in range(NSHIFT):
        row = shift_raw[n].astype(F32)
        for c in range(CH):
            for r in range(2):
                sh[c, n, r] = jnp.broadcast_to(
                    row[r : r + 1, c * KC : (c + 1) * KC], (HALF, KC)
                )

    def lift(rows, first_leaf, chunks=range(CH)):
        for c in chunks:
            moved = dot(rows, w[pl.ds(c * KC, KC), :], NT_DIMS)
            for i in range(LEAF):
                leaf = first_leaf + i
                turn = turn_s[leaf]
                s_re = sh[c, turn, 0]
                s_im = sh[c, turn, 1]
                m_re = moved[i * COMPS : i * COMPS + HALF]
                m_im = moved[i * COMPS + HALF : (i + 1) * COMPS]
                shifted[c, leaf, 0:HALF] = m_re * s_re - m_im * s_im
                shifted[c, leaf, HALF:COMPS] = m_re * s_im + m_im * s_re

    def rows_of(block):
        return block.reshape(LEAF * COMPS, KL)

    def block_of(offset):
        return lax.rem(samp + offset + SAMP, SAMP)

    lift(rows_of(own[...]), block_of(0) * LEAF)

    def near_leaf(i):
        near_copies[i].wait()
        acc = jnp.zeros((HALF, BLK), F32)
        for n in range(NEAR):
            lhs = xbuf[jnp.clip(near_s[i, n] - (flat - 1) * LEAF, 0, 3 * LEAF - 1)]
            acc += dot(lhs, jnp.concatenate([near[i, n, 0], near[i, n, 1]], axis=1), NT_DIMS)
        nearacc[i] = acc

    def expand_trans():
        trans_copy.wait()

        def body(n, carry):
            row = trans_raw[n].astype(F32)
            for c in range(CH):
                for r in range(2):
                    tr[c, n, r] = jnp.broadcast_to(
                        row[r : r + 1, c * KC : (c + 1) * KC], (HALF, KC)
                    )
            return carry

        lax.fori_loop(0, NDISP, body, 0)

    for h in range(2):
        for way in range(2):
            gathers[way, 2, h].wait_recv()
            if h == way:
                gathers[way, 4, h].start()
            gathers[way, 3, h].start()
    for dist in (2, 1, 3):
        for way in range(2):
            if dist != 2:
                gathers[way, dist, 0].wait_recv()
                if dist > 1:
                    gathers[way, dist, 1].wait_recv()
            lift(rows_of(ag[way, dist - 1]), block_of(dist if way else -dist) * LEAF)
    gathers[0, 4, 0].wait_recv()
    gathers[1, 4, 1].wait_recv()
    order_copy.wait()
    halos = []
    for c in range(CH):
        lift(rows_of(ag_f[...]), block_of(4) * LEAF, (c,))

        def sum_step(j, acc):
            keep = order_s[1, j]
            value = shifted[c, order_s[0, j]]
            acc = jnp.where(keep == 1, acc, jnp.zeros_like(acc)) + value
            seg[j] = acc
            return acc

        lax.fori_loop(0, GL, sum_step, jnp.zeros((COMPS, KC), F32), unroll=16)

        def top_step(t, carry):
            value = seg[order_s[2, t]]
            value = jnp.where(order_s[3, t] == 1, value, jnp.zeros_like(value)).astype(BF16)
            topbf[c, t] = value
            srcf[c, RIM + t] = value.astype(F32)
            return carry

        lax.fori_loop(0, TOP, top_step, 0, unroll=16)
        up = remote(
            topbf.at[c, pl.ds(TOP - RIM, RIM)],
            halo_l.at[c],
            halo_send.at[0, c],
            halo_recv.at[0, c],
            box_next,
        )
        dn = remote(
            topbf.at[c, pl.ds(0, RIM)],
            halo_r.at[c],
            halo_send.at[1, c],
            halo_recv.at[1, c],
            box_prev,
        )
        up.start()
        dn.start()
        halos.append((up, dn))
    expand_trans()

    for c in range(CH):
        halos[c][0].wait_recv()
        halos[c][1].wait_recv()

        def widen(t, carry):
            srcf[c, t] = halo_l[c, t].astype(F32)
            srcf[c, RIM + TOP + t] = halo_r[c, t].astype(F32)
            return carry

        lax.fori_loop(0, RIM, widen, 0, unroll=2)

        def move(t, carry):
            acc_re = jnp.zeros((HALF, KC), F32)
            acc_im = jnp.zeros((HALF, KC), F32)
            for j in range(ILIST):
                source = (src_s[t, j] - (box * TOP - RIM)) & (2 * TOP - 1)
                disp = disp_s[t, j]
                s_re = srcf[c, source, 0:HALF]
                s_im = srcf[c, source, HALF:COMPS]
                t_re = tr[c, disp, 0]
                t_im = tr[c, disp, 1]
                acc_re += t_re * s_re - t_im * s_im
                acc_im += t_re * s_im + t_im * s_re
            value = jnp.concatenate([acc_re, acc_im], axis=0)
            inc[t] = value.astype(BF16).astype(F32)
            return carry

        lax.fori_loop(0, TOP, move, 0, unroll=2)

        def lower(at, carry):
            leaf = lax.rem(at + samp * LEAF, GL)
            value = inc[parent_s[0, leaf] & (TOP - 1)]
            turn = turn_s[leaf]
            s_re = sh[c, turn, 0]
            s_im = sh[c, turn, 1]
            v_re, v_im = value[:HALF], value[HALF:]
            d_re = s_re * v_re + s_im * v_im
            d_im = s_re * v_im - s_im * v_re
            down[at, :, c * KC : (c + 1) * KC] = jnp.concatenate(
                [d_re, d_im], axis=0
            ).astype(BF16)
            return carry

        lax.fori_loop(0, GL, lower, 0, unroll=16)

    def far_part(first, count):
        rows = down[pl.ds(first * LEAF, count * LEAF)].reshape(count * LEAF * COMPS, KD)
        res = dot(rows, w[...], NN_DIMS).astype(BF16)
        part[pl.ds(first * LEAF, count * LEAF)] = res.reshape(count * LEAF, COMPS, KL)

    def part_half(offset, h):
        return pl.ds((offset % SAMP) * LEAF + 2 * h, 2)

    signs = (1, -1)
    relays = {}
    quarters = {}
    firsts = {}
    seconds = {}
    for way in range(2):
        quarters[way] = remote(
            part.at[part_half(4, way)],
            half_in.at[way],
            rs_send.at[way, 0, 0],
            rs_recv.at[way, 0, 0],
            twos[way],
        )
        firsts[way] = remote(
            part.at[pl.ds((signs[way] % SAMP) * LEAF, LEAF)],
            near_in.at[way],
            rs_send.at[way, 0, 1],
            rs_recv.at[way, 0, 1],
            ones[way],
        )
        for h in range(2):
            relays[way, h] = remote(
                part.at[part_half(3 * signs[way], h)],
                relay_in.at[way, half(h)],
                rs_send.at[way, 1, h],
                rs_recv.at[way, 1, h],
                ones[way],
            )
            seconds[way, h] = remote(
                relay_out.at[way, half(h)],
                end_in.at[way, half(h)],
                rs_send.at[way, 2, h],
                rs_recv.at[way, 2, h],
                twos[way],
            )

    far_part(3, 3)
    for way in range(2):
        quarters[way].start()
        relays[way, 1 - way].start()
    for way in range(2):
        relays[way, way].start()
    far_part(6, 2)
    firsts[1].start()
    far_part(1, 2)
    firsts[0].start()
    for way in range(2):
        h = 1 - way
        relays[way, h].wait_recv()
        mine = part[part_half(2 * signs[way], h)].astype(F32)
        relay_out[way, half(h)] = (mine + relay_in[way, half(h)].astype(F32)).astype(BF16)
        seconds[way, h].start()
    for way in range(2):
        h = way
        relays[way, h].wait_recv()
        quarters[way].wait_recv()
        mine = part[part_half(2 * signs[way], h)].astype(F32)
        relay_out[way, half(h)] = (
            mine + relay_in[way, half(h)].astype(F32) + half_in[way].astype(F32)
        ).astype(BF16)
        seconds[way, h].start()
    far_part(0, 1)
    cur_up.wait_recv()
    cur_dn.wait_recv()
    for m in range(3 * LEAF):
        x = nbr[m].astype(F32)
        turned = jnp.concatenate([-x[EXC:], x[:EXC]], axis=0)
        xbuf[m] = jnp.concatenate([x, turned], axis=1).astype(BF16)
    near_leaf(0)
    near_leaf(1)
    near_leaf(2)
    near_leaf(3)
    for way in range(2):
        firsts[way].wait_recv()
    for way in range(2):
        seconds[way, 1 - way].wait_recv()
    for way in range(2):
        seconds[way, way].wait_recv()

    for i in range(LEAF):
        far = (
            part[i].astype(F32)
            + (near_in[0, i].astype(F32) + near_in[1, i].astype(F32))
            + (end_in[0, i].astype(F32) + end_in[1, i].astype(F32))
        ).astype(BF16)
        cat = jnp.concatenate([rad[i, p, r] for p in range(2) for r in range(2)], axis=1)
        g = dot(far, cat, NN_DIMS)
        re = (
            g[0:4, 0:128] + g[8:12, 128:256] + g[4:8, 256:384] + g[12:16, 384:512]
        )
        im = (
            g[8:12, 0:128] - g[0:4, 128:256] + g[12:16, 256:384] - g[4:8, 384:512]
        )
        out_ref[i] = jnp.concatenate([re, im], axis=0) + nearacc[i]

    for copy in gathers.values():
        copy.wait_send()
    cur_up.wait_send()
    cur_dn.wait_send()
    for up, dn in halos:
        up.wait_send()
        dn.wait_send()
    for group in (quarters, firsts, relays, seconds):
        for copy in group.values():
            copy.wait_send()


def order_leaves(row, table):
    wide = (GL, GL)
    ups = lax.broadcasted_iota(jnp.int32, wide, 0)
    ids = lax.broadcasted_iota(jnp.int32, wide, 1)
    row = jnp.broadcast_to(row, wide)
    col = jnp.sum(jnp.where(ups == ids, row, 0), axis=1, keepdims=True)
    col = jnp.broadcast_to(col, wide)
    lower = (row * GL + ids) < (col * GL + ups)
    rank = jnp.sum(lower.astype(jnp.int32), axis=1, keepdims=True)
    rank = jnp.broadcast_to(rank, wide)
    at = rank == ids

    def total(value):
        return jnp.sum(value, axis=0, keepdims=True)

    order = total(jnp.where(at, ups, 0))
    here = total(jnp.where(at, col, 0))
    before = total(jnp.where(rank == ids - 1, col + 1, 0)) - 1
    last = jnp.maximum(total((col <= ids).astype(jnp.int32)) - 1, 0)
    has = jnp.minimum(total((col == ids).astype(jnp.int32)), 1)
    table[...] = jnp.zeros_like(table)
    table[0:1, 0:GL] = order
    table[1:2, 0:GL] = (before == here).astype(jnp.int32)
    table[2:3, 0:GL] = last
    table[3:4, 0:GL] = has


def per_device(
    currents,
    radiation,
    near_blocks,
    near_src,
    leaf_parent,
    leaf_shift,
    shift_table,
    interp_idx,
    interp_val,
    top_src,
    top_disp,
    trans_table,
):
    boxes = lax.axis_size("box")
    any_spec = pl.BlockSpec(memory_space=pl.ANY)
    dma = pltpu.SemaphoreType.DMA
    vm = pltpu.VMEM
    sm = pltpu.SMEM
    i32 = jnp.int32
    return pl.pallas_call(
        functools.partial(kernel, boxes),
        out_shape=pltpu.VMEM((LEAF, 2 * EXC, 128), F32),
        in_specs=[any_spec] * 12,
        out_specs=pl.BlockSpec(memory_space=pltpu.VMEM),
        scratch_shapes=[
            sm((1, GL), i32),
            sm((GL,), i32),
            sm((LEAF, NEAR), i32),
            sm((2, 8), i32),
            sm((TOP, ILIST), i32),
            sm((TOP, ILIST), i32),
            sm((8, 128), i32),
            vm((1, GL), i32),
            vm((8, 128), i32),
            vm((3 * LEAF, 8, 128), BF16),
            vm((3 * LEAF, 8, 256), BF16),
            vm((LEAF, 2, 2, KL, 128), BF16),
            vm((LEAF, NEAR, 2, 128, 128), BF16),
            vm((NSHIFT, 2, KD), BF16),
            vm((8, 2, 128, 128), BF16),
            vm((NDISP, 2, KD), BF16),
            vm((KD, KL), BF16),
            vm((CH, NSHIFT, 2, HALF, KC), F32),
            vm((CH, NDISP, 2, HALF, KC), F32),
            vm((LEAF, COMPS, KL), BF16),
            vm((2, 3, LEAF, COMPS, KL), BF16),
            vm((LEAF, COMPS, KL), BF16),
            vm((CH, GL, COMPS, KC), F32),
            vm((GL, COMPS, KC), F32),
            vm((CH, TOP, COMPS, KC), BF16),
            vm((CH, RIM, COMPS, KC), BF16),
            vm((CH, RIM, COMPS, KC), BF16),
            vm((CH, TOP + 2 * RIM, COMPS, KC), F32),
            vm((TOP, COMPS, KC), F32),
            vm((GL, COMPS, KD), BF16),
            vm((GL, COMPS, KL), BF16),
            vm((2, LEAF, COMPS, KL), BF16),
            vm((2, LEAF, COMPS, KL), BF16),
            vm((2, 2, COMPS, KL), BF16),
            vm((2, LEAF, COMPS, KL), BF16),
            vm((2, LEAF, COMPS, KL), BF16),
            vm((LEAF, 2 * EXC, 128), F32),
            dma((20,)),
            dma((4,)),
            dma((2, 4, 2)),
            dma((2, 4, 2)),
            dma((2, CH)),
            dma((2, CH)),
            dma((2, 3, 2)),
            dma((2, 3, 2)),
        ],
        compiler_params=pltpu.CompilerParams(collective_id=0, has_side_effects=True),
    )(leaf_parent.reshape(1, GL), leaf_shift, near_src, interp_idx.T, top_src, top_disp, currents, radiation, near_blocks, shift_table, interp_val, trans_table)


def solution(mesh):
    placed = (
        P(("box", "samp"), None, None),
        P(("box", "samp"), None, None, None, None),
        P(("box", "samp"), None, None, None, None),
        P(("box", "samp"), None),
        P("box"),
        P("box"),
        P(None, None, "samp"),
        P("samp", None),
        P("samp", None, None, None),
        P("box", None),
        P("box", None),
        P(None, None, "samp"),
    )
    return jax.shard_map(
        per_device,
        mesh=mesh,
        in_specs=placed,
        out_specs=P(("box", "samp"), None, None),
        check_vma=False,
    )
```
